32 devices in a mesh: row: 2 (over y), col: 4 (over x, core), dp: 4 (over z).
Axes of the slice: x: 2, y: 2, z: 4, core: 2. Of those that a mesh axis runs over, the one named last changes fastest.
Arguments:
- acts: bfloat16 [20480, 2560], P(('col', 'dp')), may hold values from -6 to 6
- cotangent: bfloat16 [20480, 2560], P(('col', 'dp'), 'row'), may hold values from -0.0390625 to 0.0390625
- old_weights: bfloat16 [8, 4096, 4096], P(None, 'row', ('col', 'dp')), may hold values from -0.09375 to 0.09375
- source_layer: int32 [3], replicated, may hold values from 0 to 7
- depth_coef: float32 [3], replicated, may hold values from 0.3 to 1.2
- expand_out: bfloat16 [2560, 4096], P(None, 'row'), may hold values from -0.09375 to 0.09375
- expand_in: bfloat16 [2560, 4096], P(None, ('col', 'dp')), may hold values from -0.09375 to 0.09375
Outputs:
- output: bfloat16 [20480, 2560], P(('col', 'dp'), 'row')
- in_grad: float32 [2560, 4096], P('row', ('col', 'dp'))
The draws below stay inside these ranges and needn't reach their ends.
All inputs are finite; a program needn't handle non-finite values.
Results may differ from the reference program's by a relative error of at most 0.017.
Values may be sent and summed in bfloat16 or wider, within the bound.
No kernel may reach another device: no remote copies, remote signals or barrier semaphores. Data moves between devices by JAX's collectives and lax.ppermute only.
A program may use at most 192 MiB of HBM per device.

```python
import jax
import jax.numpy as jnp

D_OLD = 4096
WIN_OUT = 2560
WIN_IN = 2560
L_OLD = 8
TOP = 3
TOKENS = 20480


def level_of(stream_key, dims, split, smallest, high):
    def one(dim, blocks):
        steps = jax.random.uniform(jax.random.fold_in(jax.random.fold_in(stream_key, 6), dim), (blocks,), jnp.float32, smallest / len(split), high / len(split))
        return jnp.repeat(jnp.exp(steps), dims[dim] // blocks).reshape((-1,) + (1,) * (len(dims) - dim - 1))

    level = one(*split[0])
    for cut in split[1:]:
        level = level * one(*cut)
    return level


def centred(rng, shape, width, limit, split=(), held_as=jnp.bfloat16):
    array = jax.random.normal(rng, shape, jnp.float32) * width
    if len(split) > 0:
        array = level_of(rng, shape, split, -0.22, 0.18) * array
    return jnp.clip(array, min=-limit, max=limit).astype(held_as)


def setup_inputs(seed: int = 0) -> dict:
    seeds = jax.random.split(jax.random.key(seed), 8)
    acts = centred(seeds[0], (TOKENS, WIN_IN), 1.0, 6.0, ((0, 16),))
    cotangent = centred(seeds[1], (TOKENS, WIN_OUT), TOKENS ** -0.5, 0.0390625, ((0, 16), (1, 2)))
    old_weights = centred(seeds[2], (L_OLD, D_OLD, D_OLD), D_OLD ** -0.5, 0.09375, ((1, 2), (2, 16)))
    source_layer = jax.random.randint(seeds[3], (TOP,), 0, L_OLD).astype(jnp.int32)
    depth_coef = jnp.clip(jax.random.uniform(seeds[4], (TOP,), jnp.float32, 0.3, 1.2), 0.3, 1.2)
    expand_out = centred(seeds[5], (WIN_OUT, D_OLD), D_OLD ** -0.5, 0.09375, ((1, 2),))
    expand_in = centred(seeds[6], (WIN_IN, D_OLD), D_OLD ** -0.5, 0.09375, ((1, 16),))
    return dict(acts=acts, cotangent=cotangent, old_weights=old_weights, source_layer=source_layer, depth_coef=depth_coef, expand_out=expand_out, expand_in=expand_in)


def reference(acts, cotangent, old_weights, source_layer, depth_coef, expand_out, expand_in):
    picks = (source_layer[:, None] == jnp.arange(L_OLD, dtype=jnp.int32)[None, :]).astype(jnp.float32)
    mixing = jnp.sum(depth_coef.astype(jnp.float32)[:, None] * picks, axis=0)
    mixed = jnp.tensordot(mixing, old_weights.astype(jnp.float32), axes=1).astype(jnp.bfloat16)
    panel = jnp.dot(expand_out, mixed, preferred_element_type=jnp.float32).astype(jnp.bfloat16)
    grown = jnp.dot(panel, expand_in.T, preferred_element_type=jnp.float32).astype(jnp.bfloat16)
    output = jnp.dot(acts, grown.T, preferred_element_type=jnp.float32).astype(jnp.bfloat16)
    weight_grad = jnp.dot(cotangent.T, acts, preferred_element_type=jnp.float32)
    in_grad = jnp.dot(weight_grad.astype(jnp.bfloat16).T, panel, preferred_element_type=jnp.float32)
    return output, in_grad
```

```python
import jax
import jax.numpy as jnp
from jax import lax
from jax.sharding import PartitionSpec as P

F32 = jnp.float32
BF16 = jnp.bfloat16


def contract_last(left, right):
    return lax.dot_general(
        left, right, (((1,), (1,)), ((), ())), preferred_element_type=F32
    )


def contract_first(left, right):
    return lax.dot_general(
        left, right, (((0,), (0,)), ((), ())), preferred_element_type=F32
    )


def general_device(acts, cotangent, old_weights, source_layer, depth_coef, expand_out, expand_in):
    layers = old_weights.shape[0]
    picks = (source_layer[:, None] == jnp.arange(layers, dtype=jnp.int32)[None, :]).astype(F32)
    mixing = jnp.sum(depth_coef[:, None] * picks, axis=0)
    mixed = jnp.tensordot(mixing, old_weights.astype(F32), axes=1).astype(BF16)
    panel = lax.psum_scatter(
        jnp.dot(expand_out, mixed, preferred_element_type=F32),
        "row",
        scatter_dimension=0,
        tiled=True,
    ).astype(BF16)
    grown = lax.psum(contract_last(panel, expand_in), ("col", "dp")).astype(BF16)
    output = contract_last(acts, grown).astype(BF16)
    summed = lax.psum(contract_first(cotangent, acts), ("col", "dp"))
    grad_low = summed.astype(BF16)
    in_grad = lax.psum_scatter(
        contract_first(grad_low, panel), "row", scatter_dimension=0, tiled=True
    )
    return (output, in_grad)


FLIP = [(0, 1), (1, 0)]
FLIP_CORE = [(k, k ^ 1) for k in range(4)]
FLIP_X = [(k, k ^ 2) for k in range(4)]
ENDS_IN = [(0, 1), (3, 2)]
MIDDLE = [(1, 2), (2, 1)]
ENDS_OUT = [(1, 0), (2, 3)]


def over_row(value):
    return lax.ppermute(value, "row", FLIP)


def over_core(value):
    return lax.ppermute(value, "col", FLIP_CORE)


def over_x(value):
    return lax.ppermute(value, "col", FLIP_X)


def cut(array, index, parts, axis):
    size = array.shape[axis] // parts
    return lax.dynamic_slice_in_dim(array, index * size, size, axis)


def add_low(left, right):
    return (left.astype(F32) + right.astype(F32)).astype(BF16)


def sum_line(value, middle):
    value = add_low(value, lax.ppermute(value, "dp", ENDS_IN))
    value = add_low(value, lax.ppermute(value, "dp", MIDDLE))
    return jnp.where(middle, value, lax.ppermute(value, "dp", ENDS_OUT))


def block_device(acts, cotangent, old_weights, source_layer, depth_coef, expand_out, expand_in):
    y = lax.axis_index("row")
    k = lax.axis_index("col")
    z = lax.axis_index("dp")
    x, c = k // 2, k % 2
    middle = jnp.logical_or(z == 1, z == 2)

    quarters = expand_in.reshape((2, 2, expand_in.shape[0] // 4, expand_in.shape[1]))
    e_x = over_x(cut(quarters, 1 - x, 2, 1))
    e_own = cut(quarters, x, 2, 1)
    e_pair = jnp.concatenate([e_own, e_x], axis=3)[:, 0]
    e_core = over_core(cut(e_pair, 1 - c, 2, 0))[0]
    e_all = jnp.concatenate([cut(e_pair, c, 2, 0)[0], e_core], axis=1)

    mixed = jnp.zeros(old_weights.shape[1:], F32)
    for term in range(source_layer.shape[0]):
        layer = lax.dynamic_index_in_dim(old_weights, source_layer[term], 0, False)
        mixed = mixed + depth_coef[term] * layer.astype(F32)
    mixed = mixed.astype(BF16)
    part = jnp.dot(expand_out, mixed, preferred_element_type=F32)
    panel = add_low(cut(part, y, 2, 0), over_row(cut(part, 1 - y, 2, 0).astype(BF16)))

    panel_pair = jnp.concatenate([panel, over_x(panel)], axis=1)
    panel_all = jnp.concatenate([panel_pair, over_core(panel_pair)], axis=1)

    cot_own, cot_other = cut(cotangent, c, 2, 1), cut(cotangent, 1 - c, 2, 1)

    def reduced(half):
        columns = cut(acts, half, 2, 1)
        sent = over_core(contract_first(cot_other, columns).astype(BF16))
        chip = (contract_first(cot_own, columns) + sent.astype(F32)).astype(BF16)
        return add_low(cut(chip, x, 2, 1), over_x(cut(chip, 1 - x, 2, 1)))

    panel_turned = jnp.concatenate([cut(panel_pair, c, 2, 0), cut(panel_pair, 1 - c, 2, 0)], axis=0)

    def grad_of(half):
        total = sum_line(reduced(half), middle)
        both = jnp.concatenate([total, over_core(total)], axis=0)
        return contract_first(both, panel_turned)

    rows = panel.shape[0] // 2
    pieces = []
    for i in range(2):
        mine = contract_last(panel_all[i * rows : (i + 1) * rows], e_all).astype(BF16)
        pieces.append(mine)

    first = grad_of(1 - y)
    first_sent = over_row(first.astype(BF16))

    outputs = []
    a_turned = jnp.concatenate(
        [cut(acts, q, 4, 1) for q in (2 * c + x, 2 * c + 1 - x, 2 - 2 * c + x, 3 - 2 * c - x)], axis=1
    )
    for i in range(2):
        total = sum_line(pieces[i], middle)
        pair = jnp.concatenate([total, over_x(total)], axis=1)
        full = jnp.concatenate([pair, over_core(pair)], axis=1)
        outputs.append(contract_last(a_turned, full).astype(BF16))
    output = jnp.concatenate(outputs, axis=1)

    second = grad_of(y) + first_sent.astype(F32)
    width = second.shape[1] // 2
    swapped = over_x(second[:, width:].astype(BF16)).astype(F32)
    kept = second[:, :width]
    in_grad = jnp.concatenate(
        [jnp.where(x == 0, kept, swapped), jnp.where(x == 0, swapped, kept)], axis=0
    )
    return (output, in_grad)


def solution(mesh):
    placed = (
        P(("col", "dp"), None),
        P(("col", "dp"), "row"),
        P(None, "row", ("col", "dp")),
        P(),
        P(),
        P(None, "row"),
        P(None, ("col", "dp")),
    )
    sizes = (mesh.shape["row"], mesh.shape["col"], mesh.shape["dp"])
    return jax.shard_map(
        block_device if sizes == (2, 4, 4) else general_device,
        mesh=mesh,
        in_specs=placed,
        out_specs=(P(("col", "dp"), "row"), P("row", ("col", "dp"))),
        check_vma=False,
    )
```
